256 devices in a mesh: dp: 32 (over y_lo, z, core), seq: 8 (over y_hi, x).
Axes of the slice: x: 4, y: 4 (y_hi: 2, y_lo: 2; y = y_hi * 2 + y_lo), z: 8, core: 2. Of those that a mesh axis runs over, the one named last changes fastest.
Arguments:
- acts: bfloat16 [32768, 4096], P(('dp', 'seq')), may hold values from -24 to 24
- grad_out: bfloat16 [32768, 4096], P('dp', 'seq'), may hold values from -6 to 6
- proj_weight: bfloat16 [4096, 4096], P('dp', 'seq'), may hold values from -0.09375 to 0.09375
Outputs:
- grad_acts: float32 [32768, 4096], P(('dp', 'seq'))
- grad_weight: float32 [4096, 4096], P('dp', 'seq')
The draws below stay inside these ranges and needn't reach their ends.
All inputs are finite; a program needn't handle non-finite values.
Results may differ from the reference program's by a relative error of at most 0.014.
Values may be sent and summed in bfloat16 or wider, within the bound.
No kernel may reach another device: no remote copies, remote signals or barrier semaphores. Data moves between devices by JAX's collectives and lax.ppermute only.
A program may use at most 64 MiB of HBM per device.

```python
import jax
import jax.numpy as jnp
from jax import lax

DI = 4096
DO = 4096
TOK_DEV = 128
TOKENS = 32768
N_DP = 32
N_SEQ = 8


def strengthened(array, rng, source, target, parts, factor):
    def block_of(position):
        return (jnp.arange(array.shape[position]) // (array.shape[position] // parts)).reshape((-1,) + (1,) * (array.ndim - 1 - position))

    one_side = jax.random.permutation(rng, parts)[block_of(target)]
    far = (block_of(target) + parts // 2) % parts
    return jnp.where((block_of(source) == one_side) | (block_of(source) == far), factor * array, array)


def steps_of(stream_key, extent, cuts, low, high):
    level, own = 1.0, jax.random.fold_in(stream_key, 6)
    for dim, shards_of in cuts:
        heights = jnp.exp(jax.random.uniform(jax.random.fold_in(own, dim), (shards_of,), jnp.float32, low / len(cuts), high / len(cuts)))
        level = level * jnp.repeat(heights, extent[dim] // shards_of).reshape([-1 if axis == dim else 1 for axis in range(len(extent))])
    return level


def noise(own_key, extent, spread, most, split=(), kind=jnp.bfloat16):
    result = spread * jax.random.normal(own_key, extent, jnp.float32)
    if split:
        result = result * steps_of(own_key, extent, split, -0.22, 0.18)
    return jnp.clip(result, -most, most).astype(kind)


def bell_draw_with(rng, extent, scale, most, pieces, heavy, held_as=jnp.bfloat16):
    entries = scale * jax.random.normal(rng, extent, jnp.float32)
    if pieces:
        entries = entries * steps_of(rng, extent, pieces, -0.22, 0.18)
    return jnp.clip(strengthened(entries, jax.random.fold_in(rng, 3), *heavy), -most, most).astype(held_as)


def setup_inputs(seed: int = 0) -> dict:
    streams_of = jax.random.split(jax.random.key(seed), 4)
    return {
        "acts": bell_draw_with(streams_of[0], (TOKENS, DI), 1.0, 24.0, ((0, 256),), (0, 1, 256, 6.0)),
        "grad_out": noise(streams_of[1], (TOKENS, DO), 1.0, 6.0, ((0, 32), (1, 8))),
        "proj_weight": noise(streams_of[2], (DI, DO), DI ** -0.5, 0.09375, ((0, 32), (1, 8))),
    }


def reference(acts, grad_out, proj_weight):
    width = DO // N_SEQ

    def add_block(index, total):
        start = (index * width).astype(jnp.int32)
        cols = lax.dynamic_slice_in_dim(grad_out, start, width, 1)
        wcols = lax.dynamic_slice_in_dim(proj_weight, start, width, 1)
        part = lax.dot_general(cols, wcols, (((1,), (1,)), ((), ())), preferred_element_type=jnp.float32)
        part = lax.optimization_barrier(part.astype(jnp.bfloat16))
        return total + part.astype(jnp.float32)
    grad_acts = lax.fori_loop(jnp.int32(0), jnp.int32(N_SEQ), add_block, jnp.zeros((TOKENS, DI), jnp.float32))
    group = TOK_DEV * N_SEQ

    def add_group(index, total):
        start = (index * group).astype(jnp.int32)
        rows_a = lax.dynamic_slice_in_dim(acts, start, group, 0)
        rows_g = lax.dynamic_slice_in_dim(grad_out, start, group, 0)
        term = lax.dot_general(rows_a, rows_g, (((0,), (0,)), ((), ())), preferred_element_type=jnp.float32)
        term = lax.optimization_barrier(term.astype(jnp.bfloat16))
        return total + term.astype(jnp.float32)
    product = lax.fori_loop(jnp.int32(0), jnp.int32(N_DP), add_group, jnp.zeros((DI, DO), jnp.float32))
    grad_weight = product / jnp.sqrt(jnp.float32(TOKENS))
    return (grad_acts, grad_weight)
```

```python
import jax
import jax.numpy as jnp
from jax import lax
from jax.sharding import Mesh, PartitionSpec as P

AXES = ("ylo", "z", "core", "yhi", "x")
SIZES = (2, 8, 2, 2, 4)
F32 = jnp.float32
BF16 = jnp.bfloat16


def from_x(value, offset):
    return lax.ppermute(value, "x", [((i + offset) % 4, i) for i in range(4)])


def swap(value, axis):
    return lax.ppermute(value, axis, [(0, 1), (1, 0)])


def rank16(ylo, core, x):
    return (ylo * 2 + core) * 4 + x


TO_BLOCK = [
    (rank16(x % 2, x // 2, (x + 2 * ylo + core) % 4), rank16(ylo, core, x))
    for ylo in range(2)
    for core in range(2)
    for x in range(4)
]
TO_OWNER = [(dst, src) for src, dst in TO_BLOCK]


def dot(a, b, contract):
    return lax.dot_general(a, b, ((contract[:1], contract[1:]), ((), ())), preferred_element_type=F32)


def per_device(acts, grad_out, weight):
    ylo, core = lax.axis_index("ylo"), lax.axis_index("core")
    yhi, x = lax.axis_index("yhi"), lax.axis_index("x")

    w = lax.ppermute(weight, ("ylo", "core", "x"), TO_BLOCK)
    w_other = swap(w, "ylo")
    w = jnp.concatenate([jnp.where(ylo == 0, w, w_other), jnp.where(ylo == 0, w_other, w)], axis=1)
    w = lax.all_gather(w, "z", axis=0, tiled=True)
    w_other = swap(w, "core")
    w_even = jnp.where(core == 0, w, w_other)
    w_odd = jnp.where(core == 0, w_other, w)

    blocks = acts.reshape(128, 2, 8, 2, 128).transpose(3, 1, 0, 2, 4).reshape(4, 128, 1024)

    def block_of(stack, k):
        return lax.dynamic_index_in_dim(stack, (x + k) % 4, 0, keepdims=False)

    half = jnp.zeros((4, 128, 1024), BF16)
    for k in range(4):
        piece = block_of(blocks, -k)
        piece = from_x(piece, k) if k else piece
        half = lax.dynamic_update_index_in_dim(half, piece, (x + k) % 4, 0)
    other = swap(half, "yhi")
    tokens = jnp.stack([jnp.where(yhi == 0, half, other), jnp.where(yhi == 0, other, half)])
    tokens = tokens.reshape(1024, 1024)

    g0 = grad_out
    g1 = from_x(g0, 1)
    g3 = from_x(g0, -1)
    g2 = jnp.concatenate([from_x(g1[:512], 1), from_x(g3[512:], -1)], axis=0)
    g = [g0, g1, g2, g3]

    terms = [dot(tokens, g_k, (0, 0)).astype(BF16) for g_k in g]
    keep = [jnp.where(core == 0, terms[0], terms[1]), jnp.where(core == 0, terms[2], terms[3])]
    give = [jnp.where(core == 0, terms[1], terms[0]), jnp.where(core == 0, terms[3], terms[2])]
    s = [(a.astype(F32) + swap(b, "core").astype(F32)).astype(BF16) for a, b in zip(keep, give)]
    keep = jnp.where(ylo == 0, s[0], s[1])
    give = jnp.where(ylo == 0, s[1], s[0])
    s = (keep.astype(F32) + swap(give, "ylo").astype(F32)).astype(BF16)
    s = lax.psum_scatter(s, "z", scatter_dimension=0, tiled=True)
    s = lax.ppermute(s, ("ylo", "core", "x"), TO_OWNER)
    grad_weight = s.astype(F32) / jnp.sqrt(F32(32768))

    part = dot(jnp.concatenate([g0, g2], axis=1), w_even, (1, 1))
    part = part + dot(jnp.concatenate([g1, g3], axis=1), w_odd, (1, 1))
    part = part.reshape(2, 512, 1024)
    give = lax.dynamic_index_in_dim(part, 1 - yhi, 0, keepdims=False).astype(BF16)
    mine = lax.dynamic_index_in_dim(part, yhi, 0, keepdims=False)
    mine = mine + swap(give, "yhi").astype(F32)
    mine = mine.reshape(4, 128, 1024)
    out = jnp.zeros((4, 128, 1024), F32)
    for k in range(4):
        piece = block_of(mine, -k)
        piece = from_x(piece.astype(BF16), k).astype(F32) if k else piece
        out = lax.dynamic_update_index_in_dim(out, piece, (x + k) % 4, 0)
    out = out.reshape(2, 2, 128, 8, 128).transpose(2, 1, 3, 0, 4).reshape(128, 4096)
    return (out, grad_weight)


def solution(mesh):
    fine = Mesh(mesh.devices.reshape(SIZES), AXES)
    rows = P(AXES, None)
    blocks = P(("ylo", "z", "core"), ("yhi", "x"))
    return jax.shard_map(
        per_device,
        mesh=fine,
        in_specs=(rows, blocks, blocks),
        out_specs=(rows, blocks),
        check_vma=False,
    )
```

```python
import jax
import jax.numpy as jnp
from jax import lax
from jax.experimental import pallas as pl
from jax.experimental.pallas import tpu as pltpu
from jax.sharding import Mesh, PartitionSpec as P

AXES = ("ylo", "z", "core", "yhi", "x")
SIZES = (2, 8, 2, 2, 4)
F32 = jnp.float32
BF16 = jnp.bfloat16
VMEM = pltpu.CompilerParams(vmem_limit_bytes=32 * 1024 * 1024)


def from_x(value, offset):
    return lax.ppermute(value, "x", [((i + offset) % 4, i) for i in range(4)])


def swap(value, axis):
    return lax.ppermute(value, axis, [(0, 1), (1, 0)])


def rank16(ylo, core, x):
    return (ylo * 2 + core) * 4 + x


def owner_pairs(flip):
    return [
        (rank16(ylo, core, x), rank16(x % 2, x // 2, (x + core + 2 * (ylo ^ flip)) % 4))
        for ylo in range(2)
        for core in range(2)
        for x in range(4)
    ]


def to_owner(value, flip):
    return lax.ppermute(value, ("ylo", "core", "x"), owner_pairs(flip))


def from_owner(value, flip):
    return lax.ppermute(value, ("ylo", "core", "x"), [(b, a) for a, b in owner_pairs(flip)])


barrier = lax.optimization_barrier


def dot(a, b, ca, cb):
    return lax.dot_general(a, b, (((ca,), (cb,)), ((), ())), preferred_element_type=F32)


ORDER = (4, 3, 5, 2, 6, 1, 7, 0)


def along_z(value, offset):
    return lax.ppermute(value, "z", [(i, (i + offset) % 8) for i in range(8)])


def lanes(pos_ref, block, place):
    z = lax.rem(pos_ref[0] + ORDER[place], 8)
    return pl.ds(pl.multiple_of(((block % 2) * 16 + z * 2 + block // 2) * 128, 128), 128)


def split_body(pos_ref, acts_ref, out_ref):
    for block in range(4):
        for place in range(8):
            out_ref[block * 128 : (block + 1) * 128, place * 128 : (place + 1) * 128] = acts_ref[:, lanes(pos_ref, block, place)]


def merge_body(pos_ref, parts_ref, out_ref):
    for block in range(4):
        rows = pl.ds(block * 128, 128)
        for place in range(8):
            cols = pl.ds(place * 128, 128)
            total = parts_ref[0, rows, cols].astype(F32) + parts_ref[1, rows, cols].astype(F32)
            out_ref[:, lanes(pos_ref, block, place)] = total


def local_call(body, pos, arg, shape, dtype):
    return pl.pallas_call(
        body,
        in_specs=[pl.BlockSpec(memory_space=pltpu.SMEM), pl.BlockSpec(memory_space=pltpu.VMEM)],
        out_specs=pl.BlockSpec(memory_space=pltpu.VMEM),
        out_shape=jax.ShapeDtypeStruct(shape, dtype),
        compiler_params=VMEM,
    )(pos, arg)


def per_device(acts, grad_out, weight):
    ylo, core = lax.axis_index("ylo"), lax.axis_index("core")
    yhi = lax.axis_index("yhi")
    pos = lax.axis_index("z").reshape(1)

    w_a, w_b = from_owner(weight, 0), from_owner(weight, 1)
    split = local_call(split_body, pos, acts, (512, 1024), BF16)
    split, w_a, w_b = barrier((split, w_a, w_b))
    w = jnp.concatenate([jnp.where(ylo == 0, w_a, w_b), jnp.where(ylo == 0, w_b, w_a)], axis=1)
    shards = {0: w}

    def gather_step(step):
        shards[step] = along_z(shards[step - 1], -1)
        shards[8 - step] = along_z(shards[(9 - step) % 8], 1)

    half = lax.all_to_all(split, "x", 0, 0, tiled=True)
    gather_step(1)
    g0, half, shards[1], shards[7] = barrier((grad_out, half, shards[1], shards[7]))

    g1, g3 = from_x(g0, 1), from_x(g0, -1)
    other = swap(half, "yhi")
    gather_step(2)
    gather_step(3)
    g1, g3, other, shards[3], shards[5] = barrier((g1, g3, other, shards[3], shards[5]))

    g2 = (from_x(g1[:512], 1), from_x(g3[512:], -1))
    last = (along_z(shards[3][:64], -1), along_z(shards[5][64:], 1))
    g2, last = barrier((g2, last))
    g2 = jnp.concatenate(g2)
    shards[4] = jnp.concatenate(last)
    w_own = jnp.concatenate([shards[place] for place in ORDER])
    tokens = jnp.zeros((2, 512, 1024), BF16)
    tokens = lax.dynamic_update_index_in_dim(tokens, half, yhi, 0)
    tokens = lax.dynamic_update_index_in_dim(tokens, other, 1 - yhi, 0)
    tokens = tokens.reshape(1024, 1024)

    first = core == 0
    g_all_own = jnp.concatenate([jnp.where(first, g0, g1), jnp.where(first, g2, g3)], axis=1)
    g_all_other = jnp.concatenate([jnp.where(first, g1, g0), jnp.where(first, g3, g2)], axis=1)

    def term(start, stop):
        rows = tokens[:, start * 128 : stop * 128]
        give = swap(dot(rows, g_all_other, 0, 0).astype(BF16), "core")
        return dot(rows, g_all_own, 0, 0) + give.astype(F32)

    far = term(0, 3)
    near = term(3, 8)
    blocks = [far[:128], far[128:256], far[256:]] + [near[i * 128 : (i + 1) * 128] for i in range(5)]
    blocks = dict(zip(ORDER, blocks))

    def sent(value, offset):
        return along_z(value.astype(BF16), offset)

    via = (sent(blocks[3], 1), sent(blocks[5], -1), sent(blocks[4][:64], 2), sent(blocks[4][64:], -2))
    w_other = swap(w_own, "core")
    part = [
        (dot(g_all_own[rows], w_own, 1, 1) + dot(g_all_other[rows], w_other, 1, 1)).astype(BF16)
        for rows in (slice(0, 512), slice(512, 1024))
    ]
    via, part = barrier((via, part))
    via_up, via_down, via_up2, via_down2 = [v.astype(F32) for v in via]
    up = blocks[2] + via_up
    down = blocks[6] + via_down
    up = sent(jnp.concatenate([up[:64] + via_up2, up[64:]]), 2)
    down = sent(jnp.concatenate([down[:64], down[64:] + via_down2]), -2)
    near = (sent(blocks[1], 1), sent(blocks[7], -1))
    sums = blocks[0]
    for value in (up, down, *near):
        sums = sums + value.astype(F32)
    sums = sums.astype(BF16)
    low, high = sums[:, :512], sums[:, 512:]
    here = to_owner(jnp.where(ylo == 0, low, high), 0)
    there = to_owner(jnp.where(ylo == 0, high, low), 1)
    grad_weight = (here.astype(F32) + there.astype(F32)) / jnp.sqrt(F32(32768))

    parts = lax.all_to_all(jnp.concatenate(part), ("yhi", "x"), 0, 0, tiled=True).reshape(2, 512, 1024)
    grad_acts = local_call(merge_body, pos, parts, (128, 4096), F32)
    return (grad_acts, grad_weight)


def solution(mesh):
    fine = Mesh(mesh.devices.reshape(SIZES), AXES)
    rows = P(AXES, None)
    blocks = P(("ylo", "z", "core"), ("yhi", "x"))
    return jax.shard_map(
        per_device,
        mesh=fine,
        in_specs=(rows, blocks, blocks),
        out_specs=(rows, blocks),
        check_vma=False,
    )
```

```python
import jax
import jax.numpy as jnp
from jax import lax
from jax.experimental import pallas as pl
from jax.experimental.pallas import tpu as pltpu
from jax.sharding import Mesh, PartitionSpec as P

AXES = ("ylo", "z", "core", "yhi", "x")
SIZES = (2, 8, 2, 2, 4)
F32 = jnp.float32
BF16 = jnp.bfloat16
VMEM = pltpu.CompilerParams(vmem_limit_bytes=32 * 1024 * 1024)


def from_x(value, offset):
    return lax.ppermute(value, "x", [((i + offset) % 4, i) for i in range(4)])


def swap(value, axis):
    return lax.ppermute(value, axis, [(0, 1), (1, 0)])


def rank16(ylo, core, x):
    return (ylo * 2 + core) * 4 + x


def owner_pairs(flip):
    return [
        (rank16(ylo, core, x), rank16(x % 2, x // 2, (x + core + 2 * (ylo ^ flip)) % 4))
        for ylo in range(2)
        for core in range(2)
        for x in range(4)
    ]


def to_owner(value, flip):
    return lax.ppermute(value, ("ylo", "core", "x"), owner_pairs(flip))


def from_owner(value, flip):
    return lax.ppermute(value, ("ylo", "core", "x"), [(b, a) for a, b in owner_pairs(flip)])


barrier = lax.optimization_barrier


def dot(a, b, ca, cb):
    return lax.dot_general(a, b, (((ca,), (cb,)), ((), ())), preferred_element_type=F32)


ORDER = (4, 3, 5, 2, 6, 1, 7, 0)


def along_z(value, offset):
    return lax.ppermute(value, "z", [(i, (i + offset) % 8) for i in range(8)])


def lanes(pos_ref, block, place):
    z = lax.rem(pos_ref[0] + ORDER[place], 8)
    return pl.ds(pl.multiple_of(((block % 2) * 16 + z * 2 + block // 2) * 128, 128), 128)


def split_body(pos_ref, acts_ref, out_ref):
    for block in range(4):
        for place in range(8):
            out_ref[block * 128 : (block + 1) * 128, place * 128 : (place + 1) * 128] = acts_ref[:, lanes(pos_ref, block, place)]


def merge_body(pos_ref, parts_ref, out_ref):
    for block in range(4):
        rows = pl.ds(block * 128, 128)
        for place in range(8):
            cols = pl.ds(place * 128, 128)
            total = parts_ref[0, rows, cols].astype(F32) + parts_ref[1, rows, cols].astype(F32)
            out_ref[:, lanes(pos_ref, block, place)] = total


def local_call(body, pos, arg, shape, dtype):
    return pl.pallas_call(
        body,
        in_specs=[pl.BlockSpec(memory_space=pltpu.SMEM), pl.BlockSpec(memory_space=pltpu.VMEM)],
        out_specs=pl.BlockSpec(memory_space=pltpu.VMEM),
        out_shape=jax.ShapeDtypeStruct(shape, dtype),
        compiler_params=VMEM,
    )(pos, arg)


def per_device(acts, grad_out, weight):
    ylo, core = lax.axis_index("ylo"), lax.axis_index("core")
    yhi = lax.axis_index("yhi")
    pos = lax.axis_index("z").reshape(1)

    w_a, w_b = from_owner(weight, 0), from_owner(weight, 1)
    split = local_call(split_body, pos, acts, (512, 1024), BF16)
    split, w_a, w_b = barrier((split, w_a, w_b))
    w = jnp.concatenate([jnp.where(ylo == 0, w_a, w_b), jnp.where(ylo == 0, w_b, w_a)], axis=1)
    shards = {0: w}

    def gather_step(step):
        shards[step] = along_z(shards[step - 1], -1)
        shards[8 - step] = along_z(shards[(9 - step) % 8], 1)

    half = lax.all_to_all(split, "x", 0, 0, tiled=True)
    gather_step(1)
    g0, half, shards[1], shards[7] = barrier((grad_out, half, shards[1], shards[7]))

    g1, g3 = from_x(g0, 1), from_x(g0, -1)
    other = swap(half, "yhi")
    gather_step(2)
    gather_step(3)
    g1, g3, other, shards[3], shards[5] = barrier((g1, g3, other, shards[3], shards[5]))

    g2 = (from_x(g1[:512], 1), from_x(g3[512:], -1))
    last = (along_z(shards[3][:64], -1), along_z(shards[5][64:], 1))
    g2, last = barrier((g2, last))
    g2 = jnp.concatenate(g2)
    shards[4] = jnp.concatenate(last)
    w_own = jnp.concatenate([shards[place] for place in ORDER])
    tokens = jnp.zeros((2, 512, 1024), BF16)
    tokens = lax.dynamic_update_index_in_dim(tokens, half, yhi, 0)
    tokens = lax.dynamic_update_index_in_dim(tokens, other, 1 - yhi, 0)
    tokens = tokens.reshape(1024, 1024)

    first = core == 0
    g_all_own = jnp.concatenate([jnp.where(first, g0, g1), jnp.where(first, g2, g3)], axis=1)
    g_all_other = jnp.concatenate([jnp.where(first, g1, g0), jnp.where(first, g3, g2)], axis=1)

    def term(start, stop):
        rows = tokens[:, start * 128 : stop * 128]
        give = swap(dot(rows, g_all_other, 0, 0).astype(BF16), "core")
        return (dot(rows, g_all_own, 0, 0) + give.astype(F32)).astype(BF16)

    whole = term(0, 8)
    blocks = [whole[i * 128 : (i + 1) * 128] for i in range(8)]
    blocks = dict(zip(ORDER, blocks))

    def sent(value, offset):
        return along_z(value.astype(BF16), offset)

    via = (sent(blocks[3], 1), sent(blocks[5], -1), sent(blocks[4][:64], 2), sent(blocks[4][64:], -2))
    w_other = swap(w_own, "core")
    part = dot(jnp.concatenate([g_all_own, g_all_other], axis=1), jnp.concatenate([w_own, w_other], axis=1), 1, 1).astype(BF16)
    via, part = barrier((via, part))
    via_up, via_down, via_up2, via_down2 = [v.astype(F32) for v in via]
    up = blocks[2].astype(F32) + via_up
    down = blocks[6].astype(F32) + via_down
    up = sent(jnp.concatenate([up[:64] + via_up2, up[64:]]), 2)
    down = sent(jnp.concatenate([down[:64], down[64:] + via_down2]), -2)
    near = (sent(blocks[1], 1), sent(blocks[7], -1))
    sums = blocks[0].astype(F32)
    for value in (up, down, *near):
        sums = sums + value.astype(F32)
    sums = sums.astype(BF16)
    low, high = sums[:, :512], sums[:, 512:]
    here = to_owner(jnp.where(ylo == 0, low, high), 0)
    there = to_owner(jnp.where(ylo == 0, high, low), 1)
    grad_weight = (here.astype(F32) + there.astype(F32)) / jnp.sqrt(F32(32768))

    parts = lax.all_to_all(part, ("yhi", "x"), 0, 0, tiled=True).reshape(2, 512, 1024)
    grad_acts = local_call(merge_body, pos, parts, (128, 4096), F32)
    return (grad_acts, grad_weight)


def solution(mesh):
    fine = Mesh(mesh.devices.reshape(SIZES), AXES)
    rows = P(AXES, None)
    blocks = P(("ylo", "z", "core"), ("yhi", "x"))
    return jax.shard_map(
        per_device,
        mesh=fine,
        in_specs=(rows, blocks, blocks),
        out_specs=(rows, blocks),
        check_vma=False,
    )
```
